512 devices in a mesh: row: 16 (over x, z_hi), col: 8 (over y), mat: 4 (over z_lo, core).
Axes of the slice: x: 4, y: 8, z: 8 (z_hi: 4, z_lo: 2; z = z_hi * 2 + z_lo), core: 2. Of those that a mesh axis runs over, the one named last changes fastest.
Arguments:
- grads: float32 [4, 4096, 4096], P('mat', 'row', 'col'), may hold values from -6 to 6
- left_stats: float32 [4, 4096, 256], P('mat', 'row'), as said below
- right_stats: float32 [4, 4096, 256], P('mat', 'col'), as said below
Outputs:
- update: float32 [4, 4096, 4096], P('mat', ('row', 'col'))
The draws below stay inside these ranges and needn't reach their ends.
Inputs may be any that keep to these rules, and one draw needn't show every extreme that they name: `left_stats`: each aligned block of 256 rows along the second dimension, taken as a 256 x 256 matrix, is symmetric positive definite. `right_stats`: each aligned block of 256 rows along the second dimension, taken as a 256 x 256 matrix, is symmetric positive definite.
All inputs are finite; a program needn't handle non-finite values.
Results may differ from the reference program's by a relative error of at most 0.00011.
Values sent between devices are 32-bit elements; how exact they have to be, the bound alone decides.
A program may use at most 64 MiB of HBM per device.

```python
import jax
import jax.numpy as jnp
from jax import lax

D = 4096
BLK = 256
ITERS = 3
MATS = 4


def spd_blocks(key):
    nblk = D // BLK
    first, second = jax.random.split(key)
    raw = jax.random.normal(first, (MATS, nblk, BLK, BLK), jnp.float32)
    prod = jnp.einsum('mibk,mick->mibc', raw, raw, precision=lax.Precision.HIGHEST) / BLK
    diag = jax.random.uniform(jax.random.fold_in(second, 3), (MATS, nblk, BLK), jnp.float32, 0.3, 2.0)
    prod = prod + diag[..., None] * jnp.eye(BLK, dtype=jnp.float32)
    return prod.reshape(MATS, D, BLK)


def draw_left_stats(key, part):
    return spd_blocks(jax.random.fold_in(key, 11))


def draw_right_stats(key, part):
    return spd_blocks(jax.random.fold_in(key, 23))


def shard_levels(stream_key, dims, pieces, least, largest):
    def one(axis_at, parts):
        steps = jax.random.uniform(jax.random.fold_in(jax.random.fold_in(stream_key, 6), axis_at), (parts,), jnp.float32, least / len(pieces), largest / len(pieces))
        return jnp.repeat(jnp.exp(steps), dims[axis_at] // parts).reshape((-1,) + (1,) * (len(dims) - axis_at - 1))

    factor_of = one(*pieces[0])
    for cut in pieces[1:]:
        factor_of = factor_of * one(*cut)
    return factor_of


def normal_values(key, dims, spread, bound, pieces=(), kind=jnp.bfloat16):
    factor_of = shard_levels(key, dims, pieces, -0.22, 0.18) if pieces else 1.0
    values = jax.random.normal(key, dims, jnp.float32) * spread * factor_of
    return jnp.minimum(jnp.maximum(values, -bound), bound).astype(kind)


def setup_inputs(seed: int = 0) -> dict:
    streams_of = jax.random.split(jax.random.key(seed), 4)
    return {
        "grads": normal_values(streams_of[0], (MATS, D, D), 1.0, 6.0, ((0, 4), (1, 16), (2, 8)), jnp.float32),
        "left_stats": draw_left_stats(jax.random.fold_in(streams_of[3], 71), 0),
        "right_stats": draw_right_stats(jax.random.fold_in(streams_of[3], 71), 0),
    }


beta_mix = 0.5
eps_shift = 0.001

def matmul(left, right):
    return jnp.einsum('...ij,...jk->...ik', left, right, precision=lax.Precision.HIGHEST)

def newton_root(factor):
    size = factor.shape[-1]
    ident = jnp.eye(size, dtype=factor.dtype)
    scale = jnp.sqrt(lax.optimization_barrier(jnp.sum(factor * factor, axis=(-2, -1), keepdims=True)))
    moving = factor / scale
    result = jnp.broadcast_to(ident, factor.shape)
    for count in range(ITERS):
        step_mat = (5.0 * ident - moving) * 0.25
        result = matmul(result, step_mat)
        squared = matmul(step_mat, step_mat)
        moving = matmul(matmul(squared, squared), moving)
    return result * jnp.power(scale, -0.25)

def reference(grads, left_stats, right_stats):
    mats = grads.shape[0]
    nblk = D // BLK
    ident = jnp.eye(BLK, dtype=grads.dtype)
    by_rows = grads.reshape(mats, nblk, BLK, D)
    left_gram = jnp.einsum('mibd,mied->mibe', by_rows, by_rows, precision=lax.Precision.HIGHEST) / D
    by_cols = grads.reshape(mats, D, nblk, BLK)
    right_gram = jnp.einsum('mdjb,mdje->mjbe', by_cols, by_cols, precision=lax.Precision.HIGHEST) / D
    left_factor = beta_mix * left_stats.reshape(mats, nblk, BLK, BLK) + (1.0 - beta_mix) * left_gram + eps_shift * ident
    right_factor = beta_mix * right_stats.reshape(mats, nblk, BLK, BLK) + (1.0 - beta_mix) * right_gram + eps_shift * ident
    left_root = newton_root(left_factor)
    right_root = newton_root(right_factor)
    half = jnp.einsum('mibe,mied->mibd', left_root, by_rows, precision=lax.Precision.HIGHEST)
    half = half.reshape(mats, D, nblk, BLK)
    full = jnp.einsum('mdjb,mjbe->mdje', half, right_root, precision=lax.Precision.HIGHEST)
    return full.reshape(mats, D, D)
```

```python
import jax
import jax.numpy as jnp
from jax import lax
from jax.experimental import pallas as pl
from jax.experimental.pallas import tpu as pltpu
from jax.sharding import PartitionSpec as P

D = 4096
BLK = 256
H = 128
NX, NZ, NY = 4, 4, 8
BETA, EPS = 0.5, 0.001
F32, BF16 = jnp.float32, jnp.bfloat16
MESH = pl.DeviceIdType.MESH
PACK = 3 * H
RP = PACK // (NX * NZ)
LP = PACK // NY
YORD = (4, 3, 5, 2, 6, 1, 7)
XORD = (2, 1, 3)
ZORD = (2, 1, 3)


def split(v):
    hi = v.astype(BF16)
    return hi, (v - hi.astype(F32)).astype(BF16)


def dot(a, b):
    return jnp.dot(a, b, preferred_element_type=F32)


def mm(a, b):
    return dot(a[0], b[0]) + (dot(a[0], b[1]) + dot(a[1], b[0]))


def pack(ref, v):
    ref[0:H, :] = v[:H, :H]
    ref[H : 2 * H, :] = v[:H, H:]
    ref[2 * H : 3 * H, :] = v[H:, H:]


def unpack(ref):
    a, b, d = ref[0:H, :], ref[H : 2 * H, :], ref[2 * H : 3 * H, :]
    top = jnp.concatenate([a, b], axis=1)
    low = jnp.concatenate([b.T, d], axis=1)
    return jnp.concatenate([top, low], axis=0)


def eye():
    rows = lax.broadcasted_iota(jnp.int32, (BLK, BLK), 0)
    cols = lax.broadcasted_iota(jnp.int32, (BLK, BLK), 1)
    return jnp.where(rows == cols, 1.0, 0.0).astype(F32)


def newton(gram, stats):
    ident = eye()
    factor = BETA * stats + ((1.0 - BETA) / D) * gram + EPS * ident
    ss = jnp.sum(jnp.sum(factor * factor, axis=0, keepdims=True), axis=1, keepdims=True)
    m0 = factor * (1.0 / jnp.sqrt(ss))
    t1 = split(1.25 * ident - 0.25 * m0)
    s1 = split(mm(t1, t1))
    q1 = split(mm(s1, s1))
    m1 = mm(q1, split(m0))
    t2 = split(1.25 * ident - 0.25 * m1)
    s2 = split(mm(t2, t2))
    x2 = mm(t1, t2)
    q2 = split(mm(s2, s2))
    y2 = split(mm(split(m1), split(x2)))
    x3 = 1.25 * x2 - 0.25 * mm(q2, y2)
    return x3, 1.0 / jnp.sqrt(jnp.sqrt(jnp.sqrt(ss)))


def kernel(
    g_hbm, ls_hbm, rs_hbm, o_ref,
    g, ls, rs, lp, rp, lrecv, xr, zs, zr, lag, rag, upd,
    in_sem, out_sem, ly_s, ly_r, lg_s, lg_r, x_s, x_r, z_s, z_r, gz_s, gz_r, gx_s, gx_r, u_s, u_r,
):
    row, col = lax.axis_index("row"), lax.axis_index("col")
    x, zh = row // NZ, lax.rem(row, NZ)

    def at_x(d):
        return lax.rem(x + d, NX)

    def at_z(e):
        return lax.rem(zh + e, NZ)

    def at_y(d):
        return lax.rem(col + d, NY)

    def to_x(d):
        return {"row": at_x(d) * NZ + zh, "col": col}

    def to_z(e):
        return {"row": x * NZ + at_z(e), "col": col}

    def to_y(d):
        return {"row": row, "col": at_y(d)}

    def send(src, dst, ss, rs_, device):
        copy = pltpu.make_async_remote_copy(
            src_ref=src, dst_ref=dst, send_sem=ss, recv_sem=rs_, device_id=device, device_id_type=MESH
        )
        copy.start()
        return copy

    loads = [
        pltpu.make_async_copy(g_hbm.at[0], g, in_sem.at[0]),
        pltpu.make_async_copy(rs_hbm.at[0], rs, in_sem.at[1]),
        pltpu.make_async_copy(ls_hbm.at[0], ls, in_sem.at[2]),
    ]
    for copy in loads:
        copy.start()
    barrier = pltpu.get_barrier_semaphore()
    greeted = [to_y(d) for d in YORD] + [to_z(e) for e in ZORD] + [to_x(d) for d in XORD]
    for device in greeted:
        pl.semaphore_signal(barrier, inc=1, device_id=device, device_id_type=MESH)

    loads[0].wait()
    tile = g[...]
    gh, gl = split(tile)
    th, tl = split(tile.T)
    for q in range(2):
        cols = slice(q * BLK, (q + 1) * BLK)
        pack(rp.at[q], mm((th[cols], tl[cols]), (gh[:, cols], gl[:, cols])))
    pack(lp, mm((gh, gl), (th, tl)))
    pl.semaphore_wait(barrier, len(greeted))

    sx, sl = {}, {}

    def right_over_x(q):
        for e in ZORD + (0,):
            for d in XORD:
                at = pl.multiple_of((at_x(d) * NZ + at_z(e)) * RP, 8)
                sx[q, d, e] = send(
                    rp.at[q, pl.ds(at, RP), :], xr.at[q, d - 1, e],
                    x_s.at[q, d - 1, e], x_r.at[q, d - 1, e], to_x(d),
                )

    right_over_x(0)
    for d in YORD:
        at = pl.multiple_of(at_y(d) * LP, 8)
        sl[d] = send(lp.at[pl.ds(at, LP), :], lrecv.at[d - 1], ly_s.at[d - 1], ly_r.at[d - 1], to_y(d))
    right_over_x(1)

    sz, kept = {}, {}
    for q in range(2):
        for e in ZORD + (0,):
            at = pl.multiple_of((x * NZ + at_z(e)) * RP, 8)
            total = rp[q, pl.ds(at, RP), :]
            for d in XORD:
                sx[q, d, e].wait_recv()
            for d in XORD:
                total = total + xr[q, d - 1, e]
            if e:
                zs[q, e - 1] = total
                sz[q, e] = send(zs.at[q, e - 1], zr.at[q, e - 1], z_s.at[q, e - 1], z_r.at[q, e - 1], to_z(e))
            else:
                kept[q] = total

    at = pl.multiple_of(col * LP, 8)
    total = lp[pl.ds(at, LP), :]
    for d in YORD:
        sl[d].wait_recv()
        total = total + lrecv[d - 1]
    lag[pl.ds(at, LP), :] = total
    sg = {}
    for d in YORD:
        sg[d] = send(lag.at[pl.ds(at, LP), :], lag.at[pl.ds(at, LP), :], lg_s.at[d - 1], lg_r.at[d - 1], to_y(d))

    gz, gx = {}, {}

    def spread_x(q, e):
        here = pl.multiple_of((x * NZ + lax.rem(zh - e + NZ, NZ)) * RP, 8)
        for d in XORD:
            gx[q, d, e] = send(
                rag.at[q, pl.ds(here, RP), :], rag.at[q, pl.ds(here, RP), :],
                gx_s.at[q, d - 1, e], gx_r.at[q, d - 1, e], to_x(d),
            )

    own = pl.multiple_of(row * RP, 8)
    for q in range(2):
        total = kept[q]
        for e in ZORD:
            sz[q, e].wait_recv()
            total = total + zr[q, e - 1]
        rag[q, pl.ds(own, RP), :] = total
        for e in ZORD:
            gz[q, e] = send(
                rag.at[q, pl.ds(own, RP), :], rag.at[q, pl.ds(own, RP), :],
                gz_s.at[q, e - 1], gz_r.at[q, e - 1], to_z(e),
            )
        spread_x(q, 0)
    for q in range(2):
        for e in (1, 3, 2):
            gz[q, e].wait_recv()
            spread_x(q, e)

    for d in YORD:
        sg[d].wait_recv()
    loads[2].wait()
    root, scale = newton(unpack(lag), ls[...])
    half = mm(split(root * scale), (gh, gl))

    loads[1].wait()
    su = {}
    for q in range(2):
        for e in range(NZ):
            for d in XORD:
                gx[q, d, e].wait_recv()
        root, scale = newton(unpack(rag.at[q]), rs[q * BLK : (q + 1) * BLK, :])
        upd[q] = mm(split(half[:, q * BLK : (q + 1) * BLK]), split(root * scale))
        lanes = pl.ds(pl.multiple_of(col * 2 * BLK + q * BLK, BLK), BLK)
        for d in YORD:
            at = pl.multiple_of(at_y(d) * 32, 32)
            su[q, d] = send(
                upd.at[q, pl.ds(at, 32), :], o_ref.at[0, :, lanes], u_s.at[q, d - 1], u_r.at[q, d - 1], to_y(d)
            )
        mine = pltpu.make_async_copy(
            upd.at[q, pl.ds(pl.multiple_of(col * 32, 32), 32), :], o_ref.at[0, :, lanes], out_sem.at[q]
        )
        mine.start()
        su[q, 0] = mine

    for q in range(2):
        su[q, 0].wait()
        for d in YORD:
            su[q, d].wait_recv()
    for group in (sx, sl, sz, sg, gz, gx):
        for copy in group.values():
            copy.wait_send()
    for (q, d), copy in su.items():
        if d:
            copy.wait_send()


def per_device(grads, left_stats, right_stats):
    dma = pltpu.SemaphoreType.DMA
    return pl.pallas_call(
        kernel,
        out_shape=jax.ShapeDtypeStruct((1, 32, D), F32),
        in_specs=[pl.BlockSpec(memory_space=pl.ANY)] * 3,
        out_specs=pl.BlockSpec(memory_space=pl.ANY),
        scratch_shapes=[
            pltpu.VMEM((BLK, 2 * BLK), F32),
            pltpu.VMEM((BLK, BLK), F32),
            pltpu.VMEM((2 * BLK, BLK), F32),
            pltpu.VMEM((PACK, H), F32),
            pltpu.VMEM((2, PACK, H), F32),
            pltpu.VMEM((NY - 1, LP, H), F32),
            pltpu.VMEM((2, NX - 1, NZ, RP, H), F32),
            pltpu.VMEM((2, NZ - 1, RP, H), F32),
            pltpu.VMEM((2, NZ - 1, RP, H), F32),
            pltpu.VMEM((PACK, H), F32),
            pltpu.VMEM((2, PACK, H), F32),
            pltpu.VMEM((2, BLK, BLK), F32),
            dma((3,)), dma((2,)),
            dma((NY - 1,)), dma((NY - 1,)), dma((NY - 1,)), dma((NY - 1,)),
            dma((2, NX - 1, NZ)), dma((2, NX - 1, NZ)),
            dma((2, NZ - 1)), dma((2, NZ - 1)), dma((2, NZ - 1)), dma((2, NZ - 1)),
            dma((2, NX - 1, NZ)), dma((2, NX - 1, NZ)),
            dma((2, NY - 1)), dma((2, NY - 1)),
        ],
        compiler_params=pltpu.CompilerParams(collective_id=0, has_side_effects=True),
        name="shampoo",
    )(grads, left_stats, right_stats)


def solution(mesh):
    return jax.shard_map(
        per_device,
        mesh=mesh,
        in_specs=(P("mat", "row", "col"), P("mat", "row", None), P("mat", "col", None)),
        out_specs=P("mat", ("row", "col"), None),
        check_vma=False,
    )
```

```python
import jax
import jax.numpy as jnp
from jax import lax
from jax.experimental import pallas as pl
from jax.experimental.pallas import tpu as pltpu
from jax.sharding import PartitionSpec as P

D = 4096
BLK = 256
H = 128
NX, NZ, NY = 4, 4, 8
BETA, EPS = 0.5, 0.001
F32, BF16 = jnp.float32, jnp.bfloat16
MESH = pl.DeviceIdType.MESH
PACK = 3 * H
XP = PACK // NX
NCH = 2
CR = XP // NCH
LP = PACK // NY
YORD = (4, 3, 5, 2, 6, 1, 7)
XORD = (2, 1, 3)
ZORD = (2, 1, 3)


def split(v):
    hi = v.astype(BF16)
    return hi, (v - hi.astype(F32)).astype(BF16)


def dot(a, b):
    return jnp.dot(a, b, preferred_element_type=F32)


def mm(a, b):
    return dot(a[0], b[0]) + (dot(a[0], b[1]) + dot(a[1], b[0]))


def pack(ref, v):
    ref[0:H, :] = v[:H, :H]
    ref[H : 2 * H, :] = v[:H, H:]
    ref[2 * H : 3 * H, :] = v[H:, H:]


def unpack(ref):
    a, b, d = ref[0:H, :], ref[H : 2 * H, :], ref[2 * H : 3 * H, :]
    top = jnp.concatenate([a, b], axis=1)
    low = jnp.concatenate([b.T, d], axis=1)
    return jnp.concatenate([top, low], axis=0)


def eye():
    rows = lax.broadcasted_iota(jnp.int32, (BLK, BLK), 0)
    cols = lax.broadcasted_iota(jnp.int32, (BLK, BLK), 1)
    return jnp.where(rows == cols, 1.0, 0.0).astype(F32)


def newton(*pairs):
    ident = eye()
    factors = [BETA * stats + ((1.0 - BETA) / D) * gram + EPS * ident for gram, stats in pairs]
    ss = [jnp.sum(jnp.sum(f * f, axis=0, keepdims=True), axis=1, keepdims=True) for f in factors]
    m0 = [f * (1.0 / jnp.sqrt(s)) for f, s in zip(factors, ss)]
    t1 = [split(1.25 * ident - 0.25 * m) for m in m0]
    s1 = [split(mm(t, t)) for t in t1]
    q1 = [split(mm(s, s)) for s in s1]
    m1 = [mm(q, split(m)) for q, m in zip(q1, m0)]
    t2 = [split(1.25 * ident - 0.25 * m) for m in m1]
    s2 = [split(mm(t, t)) for t in t2]
    x2 = [mm(a, b) for a, b in zip(t1, t2)]
    q2 = [split(mm(s, s)) for s in s2]
    y2 = [split(mm(split(m), split(v))) for m, v in zip(m1, x2)]
    x3 = [1.25 * v - 0.25 * mm(q, y) for v, q, y in zip(x2, q2, y2)]
    return [v * (1.0 / jnp.sqrt(jnp.sqrt(jnp.sqrt(s)))) for v, s in zip(x3, ss)]


def kernel(
    g_hbm, ls_hbm, rs_hbm, o_ref,
    g, ls, rs, gs, lp, rp, lrecv, xr, zs, zr, lag, rag, upd,
    in_sem, out_sem, ly_s, ly_r, lg_s, lg_r, x_s, x_r, z_s, z_r, gx_s, gx_r, u_s, u_r,
):
    row, col = lax.axis_index("row"), lax.axis_index("col")
    x, zh = row // NZ, lax.rem(row, NZ)

    def at_x(d):
        return lax.rem(x + d, NX)

    def at_z(e):
        return lax.rem(zh + e, NZ)

    def at_y(d):
        return lax.rem(col + d, NY)

    def to_x(d):
        return {"row": at_x(d) * NZ + zh, "col": col}

    def to_z(e):
        return {"row": x * NZ + at_z(e), "col": col}

    def to_y(d):
        return {"row": row, "col": at_y(d)}

    def send(src, dst, ss, rs_, device):
        copy = pltpu.make_async_remote_copy(
            src_ref=src, dst_ref=dst, send_sem=ss, recv_sem=rs_, device_id=device, device_id_type=MESH
        )
        copy.start()
        return copy

    loads = [
        pltpu.make_async_copy(g_hbm.at[0], g, in_sem.at[0]),
        pltpu.make_async_copy(rs_hbm.at[0], rs, in_sem.at[1]),
        pltpu.make_async_copy(ls_hbm.at[0], ls, in_sem.at[2]),
    ]
    for copy in loads:
        copy.start()
    barrier = pltpu.get_barrier_semaphore()
    greeted = [to_y(d) for d in YORD] + [to_z(e) for e in ZORD] + [to_x(d) for d in XORD]
    for device in greeted:
        pl.semaphore_signal(barrier, inc=1, device_id=device, device_id_type=MESH)

    sx, sl = {}, {}

    def right_over_x(q):
        for k in range(NCH):
            for d in XORD:
                at = pl.multiple_of(at_x(d) * XP + k * CR, 8)
                sx[q, k, d] = send(
                    rp.at[q, pl.ds(at, CR), :], xr.at[q, k, d - 1],
                    x_s.at[q, k, d - 1], x_r.at[q, k, d - 1], to_x(d),
                )

    loads[0].wait()
    tile = g[...]
    gh, gl = split(tile)
    th, tl = split(tile.T)
    gs[0], gs[1] = gh, gl

    def right_gram(q):
        cols = slice(q * BLK, (q + 1) * BLK)
        pack(rp.at[q], mm((th[cols], tl[cols]), (gh[:, cols], gl[:, cols])))

    right_gram(0)
    pl.semaphore_wait(barrier, len(greeted))
    right_over_x(0)
    pack(lp, mm((gh, gl), (th, tl)))
    for d in YORD:
        at = pl.multiple_of(at_y(d) * LP, 8)
        sl[d] = send(lp.at[pl.ds(at, LP), :], lrecv.at[d - 1], ly_s.at[d - 1], ly_r.at[d - 1], to_y(d))
    right_gram(1)
    right_over_x(1)

    sz = {}

    def right_over_z(q):
        for k in range(NCH):
            total = rp[q, pl.ds(pl.multiple_of(x * XP + k * CR, 8), CR), :]
            for d in XORD:
                sx[q, k, d].wait_recv()
                total = total + xr[q, k, d - 1]
            zs[q, k] = total
            for e in ZORD:
                sz[q, k, e] = send(
                    zs.at[q, k], zr.at[q, k, e - 1], z_s.at[q, k, e - 1], z_r.at[q, k, e - 1], to_z(e)
                )

    gx = {}

    def right_gather(q):
        for k in range(NCH):
            total = zs[q, k]
            for e in (1, 3, 2):
                sz[q, k, e].wait_recv()
                total = total + zr[q, k, e - 1]
            here = pl.ds(pl.multiple_of(x * XP + k * CR, 8), CR)
            rag[q, here, :] = total
            for d in XORD:
                gx[q, k, d] = send(
                    rag.at[q, here, :], rag.at[q, here, :], gx_s.at[q, k, d - 1], gx_r.at[q, k, d - 1], to_x(d)
                )

    right_over_z(0)
    right_over_z(1)

    at = pl.multiple_of(col * LP, 8)
    total = lp[pl.ds(at, LP), :]
    for d in YORD:
        sl[d].wait_recv()
        total = total + lrecv[d - 1]
    lag[pl.ds(at, LP), :] = total
    sg = {}
    for d in YORD:
        sg[d] = send(lag.at[pl.ds(at, LP), :], lag.at[pl.ds(at, LP), :], lg_s.at[d - 1], lg_r.at[d - 1], to_y(d))

    def left_arrived():
        for d in YORD:
            sg[d].wait_recv()

    def right_arrived(q):
        for k in range(NCH):
            for d in XORD:
                gx[q, k, d].wait_recv()

    def stats_of(q):
        return unpack(rag.at[q]), rs[q * BLK : (q + 1) * BLK, :]

    su = {}

    def emit(q, root):
        cols = slice(q * BLK, (q + 1) * BLK)
        upd[q] = mm(split(half(cols)), split(root))
        lanes = pl.ds(pl.multiple_of(col * 2 * BLK + q * BLK, BLK), BLK)
        for d in YORD:
            at = pl.multiple_of(at_y(d) * 32, 32)
            su[q, d] = send(
                upd.at[q, pl.ds(at, 32), :], o_ref.at[0, :, lanes], u_s.at[q, d - 1], u_r.at[q, d - 1], to_y(d)
            )
        mine = pltpu.make_async_copy(
            upd.at[q, pl.ds(pl.multiple_of(col * 32, 32), 32), :], o_ref.at[0, :, lanes], out_sem.at[q]
        )
        mine.start()
        su[q, 0] = mine

    loads[1].wait()
    loads[2].wait()
    right_gather(0)
    right_gather(1)
    left_arrived()
    right_arrived(0)
    left, right = newton((unpack(lag), ls[...]), stats_of(0))
    left = split(left)

    def half(cols):
        return mm(left, (gs[0, :, cols], gs[1, :, cols]))

    emit(0, right)
    right_arrived(1)
    (right,) = newton(stats_of(1))
    emit(1, right)

    for q in range(2):
        su[q, 0].wait()
        for d in YORD:
            su[q, d].wait_recv()
    for group in (sx, sl, sz, sg, gx):
        for copy in group.values():
            copy.wait_send()
    for (q, d), copy in su.items():
        if d:
            copy.wait_send()


def per_device(grads, left_stats, right_stats):
    dma = pltpu.SemaphoreType.DMA
    return pl.pallas_call(
        kernel,
        out_shape=pltpu.VMEM((1, 32, D), F32),
        in_specs=[pl.BlockSpec(memory_space=pl.ANY)] * 3,
        out_specs=pl.BlockSpec(memory_space=pltpu.VMEM),
        scratch_shapes=[
            pltpu.VMEM((BLK, 2 * BLK), F32),
            pltpu.VMEM((BLK, BLK), F32),
            pltpu.VMEM((2 * BLK, BLK), F32),
            pltpu.VMEM((2, BLK, 2 * BLK), BF16),
            pltpu.VMEM((PACK, H), F32),
            pltpu.VMEM((2, PACK, H), F32),
            pltpu.VMEM((NY - 1, LP, H), F32),
            pltpu.VMEM((2, NCH, NX - 1, CR, H), F32),
            pltpu.VMEM((2, NCH, CR, H), F32),
            pltpu.VMEM((2, NCH, NZ - 1, CR, H), F32),
            pltpu.VMEM((PACK, H), F32),
            pltpu.VMEM((2, PACK, H), F32),
            pltpu.VMEM((2, BLK, BLK), F32),
            dma((3,)), dma((2,)),
            dma((NY - 1,)), dma((NY - 1,)), dma((NY - 1,)), dma((NY - 1,)),
            dma((2, NCH, NX - 1)), dma((2, NCH, NX - 1)),
            dma((2, NCH, NZ - 1)), dma((2, NCH, NZ - 1)),
            dma((2, NCH, NX - 1)), dma((2, NCH, NX - 1)),
            dma((2, NY - 1)), dma((2, NY - 1)),
        ],
        compiler_params=pltpu.CompilerParams(collective_id=0, has_side_effects=True),
        name="shampoo",
    )(grads, left_stats, right_stats)


def solution(mesh):
    return jax.shard_map(
        per_device,
        mesh=mesh,
        in_specs=(P("mat", "row", "col"), P("mat", "row", None), P("mat", "col", None)),
        out_specs=P("mat", ("row", "col"), None),
        check_vma=False,
    )
```

```python
import jax
import jax.numpy as jnp
from jax import lax
from jax.experimental import pallas as pl
from jax.experimental.pallas import tpu as pltpu
from jax.sharding import PartitionSpec as P

D = 4096
BLK = 256
H = 128
NX, NZ, NY = 4, 4, 8
BETA, EPS = 0.5, 0.001
F32, BF16 = jnp.float32, jnp.bfloat16
MESH = pl.DeviceIdType.MESH
PACK = 2 * H + 8
XS, YS = 2 * H // NX, 2 * H // NY
CR, LP = XS + 8, YS + 8
NCH = 1
YORD = (4, 3, 5, 2, 6, 1, 7)
XORD = (2, 1, 3)
ZORD = (2, 1, 3)


def split(v):
    hi = v.astype(BF16)
    return hi, (v - hi.astype(F32)).astype(BF16)


def dot(a, b):
    return jnp.dot(a, b, preferred_element_type=F32)


def mm(a, b):
    return dot(a[0], b[0]) + (dot(a[0], b[1]) + dot(a[1], b[0]))


def pack(ref, v):
    rows, cols = index(H)
    low = v[H:, H:]
    ref[0:H, :] = v[:H, H:]
    ref[H : 2 * H, :] = jnp.where(rows >= cols, v[:H, :H], low)
    diagonal = jnp.sum(jnp.where(rows == cols, low, 0.0), axis=0, keepdims=True)
    ref[2 * H : PACK, :] = jnp.broadcast_to(diagonal, (8, H))


def unpack(pieces, step):
    count = pieces.shape[0]
    lines = jnp.concatenate([pieces[i, 0:step, :] for i in range(count)], axis=0)
    diagonal = pieces[count - 1, step : step + 1, :]
    rows, cols = index(H)
    b, both = lines[:H], lines[H:]
    turned = both.T
    a = jnp.where(rows >= cols, both, turned)
    d = jnp.where(rows < cols, both, jnp.where(rows > cols, turned, diagonal))
    top = jnp.concatenate([a, b], axis=1)
    low = jnp.concatenate([b.T, d], axis=1)
    return jnp.concatenate([top, low], axis=0)


def index(size):
    return (
        lax.broadcasted_iota(jnp.int32, (size, size), 0),
        lax.broadcasted_iota(jnp.int32, (size, size), 1),
    )


def eye():
    rows, cols = index(BLK)
    return jnp.where(rows == cols, 1.0, 0.0).astype(F32)


def newton(*pairs):
    ident = eye()
    factors = [BETA * stats + ((1.0 - BETA) / D) * gram + EPS * ident for gram, stats in pairs]
    ss = [jnp.sum(jnp.sum(f * f, axis=0, keepdims=True), axis=1, keepdims=True) for f in factors]
    m0 = [f * (1.0 / jnp.sqrt(s)) for f, s in zip(factors, ss)]
    t1 = [split(1.25 * ident - 0.25 * m) for m in m0]
    s1 = [split(mm(t, t)) for t in t1]
    q1 = [split(mm(s, s)) for s in s1]
    m1 = [mm(q, split(m)) for q, m in zip(q1, m0)]
    t2 = [split(1.25 * ident - 0.25 * m) for m in m1]
    s2 = [split(mm(t, t)) for t in t2]
    x2 = [mm(a, b) for a, b in zip(t1, t2)]
    q2 = [split(mm(s, s)) for s in s2]
    y2 = [split(mm(split(m), split(v))) for m, v in zip(m1, x2)]
    x3 = [1.25 * v - 0.25 * mm(q, y) for v, q, y in zip(x2, q2, y2)]
    return [v * (1.0 / jnp.sqrt(jnp.sqrt(jnp.sqrt(s)))) for v, s in zip(x3, ss)]


def kernel(
    g_hbm, ls_hbm, rs_hbm, o_ref,
    g, ls, rs, gs, hs, rr, lp, rp, lrecv, xr, zs, zr, lag, rag, upd,
    go_sem, in_sem, out_sem, ly_s, ly_r, lg_s, lg_r, x_s, x_r, z_s, z_r, gx_s, gx_r, u_s, u_r,
):
    row, col, mat = lax.axis_index("row"), lax.axis_index("col"), lax.axis_index("mat")
    core = lax.rem(mat, 2)
    twin = {"row": row, "col": col, "mat": mat + 1 - 2 * core}
    x, zh = row // NZ, lax.rem(row, NZ)

    def at_x(d):
        return lax.rem(x + d, NX)

    def at_z(e):
        return lax.rem(zh + e, NZ)

    def at_y(d):
        return lax.rem(col + d, NY)

    def to_x(d):
        return {"row": at_x(d) * NZ + zh, "col": col}

    def to_z(e):
        return {"row": x * NZ + at_z(e), "col": col}

    def to_y(d):
        return {"row": row, "col": at_y(d)}

    def remote(src, dst, ss, rs_, device):
        return pltpu.make_async_remote_copy(
            src_ref=src, dst_ref=dst, send_sem=ss, recv_sem=rs_, device_id=device, device_id_type=MESH
        )

    def send(src, dst, ss, rs_, device):
        copy = remote(src, dst, ss, rs_, device)
        copy.start()
        return copy

    loads = [
        pltpu.make_async_copy(g_hbm.at[0], g, in_sem.at[0]),
        pltpu.make_async_copy(rs_hbm.at[0], rs, in_sem.at[1]),
        pltpu.make_async_copy(ls_hbm.at[0], ls, in_sem.at[2]),
    ]
    for copy in loads:
        copy.start()
    barrier = pltpu.get_barrier_semaphore()
    greeted = [to_y(d) for d in YORD] + [to_z(e) for e in ZORD] + [to_x(d) for d in XORD] + [twin]
    for device in greeted:
        pl.semaphore_signal(barrier, inc=1, device_id=device, device_id_type=MESH)

    sx, sl = {}, {}

    def right_over_x(q):
        for k in range(NCH):
            for d in XORD:
                at = pl.multiple_of(at_x(d) * XS, 8)
                sx[q, k, d] = remote(
                    rp.at[q, pl.ds(at, CR), :], xr.at[q, k, d - 1],
                    x_s.at[q, k, d - 1], x_r.at[q, k, d - 1], to_x(d),
                )

    loads[0].wait()
    tile = g[...]
    gh, gl = split(tile)
    th, tl = split(tile.T)
    gs[0], gs[1] = gh, gl

    def right_gram(q):
        cols = slice(q * BLK, (q + 1) * BLK)
        pack(rp.at[q], mm((th[cols], tl[cols]), (gh[:, cols], gl[:, cols])))

    def start_x(q):
        for d in XORD:
            sx[q, 0, d].start()

    right_over_x(0)
    right_over_x(1)
    right_gram(0)
    pl.semaphore_wait(barrier, len(greeted))
    pl.when(core == 1)(lambda: start_x(0))
    pack(lp, mm((gh, gl), (th, tl)))
    for d in YORD:
        at = pl.multiple_of(at_y(d) * YS, 8)
        sl[d] = send(lp.at[pl.ds(at, LP), :], lrecv.at[d - 1], ly_s.at[d - 1], ly_r.at[d - 1], to_y(d))
    right_gram(1)
    pl.when(core == 0)(lambda: pl.semaphore_wait(go_sem, 1))
    pl.when(core == 0)(lambda: start_x(0))
    start_x(1)

    sz = {}

    def right_over_z(q):
        for k in range(NCH):
            total = rp[q, pl.ds(pl.multiple_of(x * XS, 8), CR), :]
            for d in XORD:
                sx[q, k, d].wait_recv()
                total = total + xr[q, k, d - 1]
            zs[q, k] = total
            for e in ZORD:
                sz[q, k, e] = send(
                    zs.at[q, k], zr.at[q, k, e - 1], z_s.at[q, k, e - 1], z_r.at[q, k, e - 1], to_z(e)
                )

    gx = {}

    def right_gather(q):
        for k in range(NCH):
            total = zs[q, k]
            for e in (1, 3, 2):
                sz[q, k, e].wait_recv()
                total = total + zr[q, k, e - 1]
            rag[q, x] = total
            for d in XORD:
                gx[q, k, d] = send(
                    rag.at[q, x], rag.at[q, x], gx_s.at[q, k, d - 1], gx_r.at[q, k, d - 1], to_x(d)
                )

    right_over_z(0)

    @pl.when(core == 1)
    def _():
        pl.semaphore_signal(go_sem, inc=1, device_id=twin, device_id_type=MESH)

    right_over_z(1)

    at = pl.multiple_of(col * YS, 8)
    total = lp[pl.ds(at, LP), :]
    for d in YORD:
        sl[d].wait_recv()
        total = total + lrecv[d - 1]
    lag[col] = total
    sg = {}
    for d in YORD:
        sg[d] = send(lag.at[col], lag.at[col], lg_s.at[d - 1], lg_r.at[d - 1], to_y(d))

    def left_arrived():
        for d in YORD:
            sg[d].wait_recv()

    def right_arrived(q):
        for k in range(NCH):
            for d in XORD:
                gx[q, k, d].wait_recv()

    def stats_of(q):
        return unpack(rag.at[q], XS), rs[q * BLK : (q + 1) * BLK, :]

    su = {}

    def emit(q, root):
        cols = slice(q * BLK, (q + 1) * BLK)
        upd[q] = mm(split(hs[:, cols]), split(root))
        lanes = pl.ds(pl.multiple_of(col * 2 * BLK + q * BLK, BLK), BLK)
        for d in YORD:
            at = pl.multiple_of(at_y(d) * 32, 32)
            su[q, d] = send(
                upd.at[q, pl.ds(at, 32), :], o_ref.at[0, :, lanes], u_s.at[q, d - 1], u_r.at[q, d - 1], to_y(d)
            )
        mine = pltpu.make_async_copy(
            upd.at[q, pl.ds(pl.multiple_of(col * 32, 32), 32), :], o_ref.at[0, :, lanes], out_sem.at[q]
        )
        mine.start()
        su[q, 0] = mine

    loads[1].wait()
    loads[2].wait()
    right_gather(0)

    @pl.when(core == 0)
    def _():
        left_arrived()
        (left,) = newton((unpack(lag, YS), ls[...]))
        hs[...] = mm(split(left), (gs[0], gs[1]))

    right_gather(1)
    right_arrived(0)

    @pl.when(core == 0)
    def _():
        (rr[...],) = newton(stats_of(0))

    @pl.when(core == 1)
    def _():
        left_arrived()
        left, rr[...] = newton((unpack(lag, YS), ls[...]), stats_of(0))
        hs[...] = mm(split(left), (gs[0], gs[1]))

    emit(0, rr[...])
    right_arrived(1)
    (right,) = newton(stats_of(1))
    emit(1, right)

    for q in range(2):
        su[q, 0].wait()
        for d in YORD:
            su[q, d].wait_recv()
    for group in (sx, sl, sz, sg, gx):
        for copy in group.values():
            copy.wait_send()
    for (q, d), copy in su.items():
        if d:
            copy.wait_send()


def per_device(grads, left_stats, right_stats):
    dma = pltpu.SemaphoreType.DMA
    return pl.pallas_call(
        kernel,
        out_shape=pltpu.VMEM((1, 32, D), F32),
        in_specs=[pl.BlockSpec(memory_space=pl.ANY)] * 3,
        out_specs=pl.BlockSpec(memory_space=pltpu.VMEM),
        scratch_shapes=[
            pltpu.VMEM((BLK, 2 * BLK), F32),
            pltpu.VMEM((BLK, BLK), F32),
            pltpu.VMEM((2 * BLK, BLK), F32),
            pltpu.VMEM((2, BLK, 2 * BLK), BF16),
            pltpu.VMEM((BLK, 2 * BLK), F32),
            pltpu.VMEM((BLK, BLK), F32),
            pltpu.VMEM((PACK, H), F32),
            pltpu.VMEM((2, PACK, H), F32),
            pltpu.VMEM((NY - 1, LP, H), F32),
            pltpu.VMEM((2, NCH, NX - 1, CR, H), F32),
            pltpu.VMEM((2, NCH, CR, H), F32),
            pltpu.VMEM((2, NCH, NZ - 1, CR, H), F32),
            pltpu.VMEM((NY, LP, H), F32),
            pltpu.VMEM((2, NX, CR, H), F32),
            pltpu.VMEM((2, BLK, BLK), F32),
            pltpu.SemaphoreType.REGULAR,
            dma((3,)), dma((2,)),
            dma((NY - 1,)), dma((NY - 1,)), dma((NY - 1,)), dma((NY - 1,)),
            dma((2, NCH, NX - 1)), dma((2, NCH, NX - 1)),
            dma((2, NCH, NZ - 1)), dma((2, NCH, NZ - 1)),
            dma((2, NCH, NX - 1)), dma((2, NCH, NX - 1)),
            dma((2, NY - 1)), dma((2, NY - 1)),
        ],
        compiler_params=pltpu.CompilerParams(collective_id=0, has_side_effects=True),
        name="shampoo",
    )(grads, left_stats, right_stats)


def solution(mesh):
    return jax.shard_map(
        per_device,
        mesh=mesh,
        in_specs=(P("mat", "row", "col"), P("mat", "row", None), P("mat", "col", None)),
        out_specs=P("mat", ("row", "col"), None),
        check_vma=False,
    )
```

```python
import jax
import jax.numpy as jnp
from jax import lax
from jax.experimental import pallas as pl
from jax.experimental.pallas import tpu as pltpu
from jax.sharding import PartitionSpec as P

D = 4096
BLK = 256
H = 128
NX, NZ, NY = 4, 4, 8
BETA, EPS = 0.5, 0.001
F32, BF16 = jnp.float32, jnp.bfloat16
MESH = pl.DeviceIdType.MESH
PACK = 2 * H + 8
XS, YS = 2 * H // NX, 2 * H // NY
CR, LP = XS + 8, YS + 8
NCH = 1
YORD = (4, 3, 5, 2, 6, 1, 7)
XORD = (2, 1, 3)
ZORD = (2, 1, 3)


def split(v):
    hi = v.astype(BF16)
    return hi, (v - hi.astype(F32)).astype(BF16)


def dot(a, b):
    return jnp.dot(a, b, preferred_element_type=F32)


def mm(a, b):
    return dot(a[0], b[0]) + (dot(a[0], b[1]) + dot(a[1], b[0]))


def pack(ref, v):
    rows, cols = index(H)
    low = v[H:, H:]
    ref[0:H, :] = v[:H, H:]
    ref[H : 2 * H, :] = jnp.where(rows >= cols, v[:H, :H], low)
    diagonal = jnp.sum(jnp.where(rows == cols, low, 0.0), axis=0, keepdims=True)
    ref[2 * H : PACK, :] = jnp.broadcast_to(diagonal, (8, H))


def unpack(pieces, step):
    count = pieces.shape[0]
    lines = jnp.concatenate([pieces[i, 0:step, :] for i in range(count)], axis=0)
    diagonal = pieces[count - 1, step : step + 1, :]
    rows, cols = index(H)
    b, both = lines[:H], lines[H:]
    turned = both.T
    a = jnp.where(rows >= cols, both, turned)
    d = jnp.where(rows < cols, both, jnp.where(rows > cols, turned, diagonal))
    top = jnp.concatenate([a, b], axis=1)
    low = jnp.concatenate([b.T, d], axis=1)
    return jnp.concatenate([top, low], axis=0)


def index(size):
    return (
        lax.broadcasted_iota(jnp.int32, (size, size), 0),
        lax.broadcasted_iota(jnp.int32, (size, size), 1),
    )


def eye():
    rows, cols = index(BLK)
    return jnp.where(rows == cols, 1.0, 0.0).astype(F32)


def newton(*pairs):
    ident = eye()
    factors = [BETA * stats + ((1.0 - BETA) / D) * gram + EPS * ident for gram, stats in pairs]
    ss = [jnp.sum(jnp.sum(f * f, axis=0, keepdims=True), axis=1, keepdims=True) for f in factors]
    m0 = [f * (1.0 / jnp.sqrt(s)) for f, s in zip(factors, ss)]
    t1 = [split(1.25 * ident - 0.25 * m) for m in m0]
    s1 = [split(mm(t, t)) for t in t1]
    q1 = [split(mm(s, s)) for s in s1]
    m1 = [mm(q, split(m)) for q, m in zip(q1, m0)]
    t2 = [split(1.25 * ident - 0.25 * m) for m in m1]
    s2 = [split(mm(t, t)) for t in t2]
    x2 = [mm(a, b) for a, b in zip(t1, t2)]
    q2 = [split(mm(s, s)) for s in s2]
    y2 = [split(mm(split(m), split(v))) for m, v in zip(m1, x2)]
    x3 = [1.25 * v - 0.25 * mm(q, y) for v, q, y in zip(x2, q2, y2)]
    return [v * (1.0 / jnp.sqrt(jnp.sqrt(jnp.sqrt(s)))) for v, s in zip(x3, ss)]


def kernel(
    g_hbm, ls_hbm, rs_hbm, o_ref,
    g, ls, rs, gs, hs, rr, lp, rp, lrecv, xr, zs, zr, lag, rag, upd,
    go_sem, in_sem, out_sem, ly_s, ly_r, lg_s, lg_r, x_s, x_r, z_s, z_r, gx_s, gx_r, u_s, u_r,
):
    row, col, mat = lax.axis_index("row"), lax.axis_index("col"), lax.axis_index("mat")
    core = lax.rem(mat, 2)
    twin = {"row": row, "col": col, "mat": mat + 1 - 2 * core}
    x, zh = row // NZ, lax.rem(row, NZ)

    def at_x(d):
        return lax.rem(x + d, NX)

    def at_z(e):
        return lax.rem(zh + e, NZ)

    def at_y(d):
        return lax.rem(col + d, NY)

    def to_x(d):
        return {"row": at_x(d) * NZ + zh, "col": col}

    def to_z(e):
        return {"row": x * NZ + at_z(e), "col": col}

    def to_y(d):
        return {"row": row, "col": at_y(d)}

    def remote(src, dst, ss, rs_, device):
        return pltpu.make_async_remote_copy(
            src_ref=src, dst_ref=dst, send_sem=ss, recv_sem=rs_, device_id=device, device_id_type=MESH
        )

    def send(src, dst, ss, rs_, device):
        copy = remote(src, dst, ss, rs_, device)
        copy.start()
        return copy

    loads = [
        pltpu.make_async_copy(g_hbm.at[0, :, 0:BLK], g.at[:, 0:BLK], in_sem.at[0]),
        pltpu.make_async_copy(g_hbm.at[0, :, BLK : 2 * BLK], g.at[:, BLK : 2 * BLK], in_sem.at[3]),
        pltpu.make_async_copy(rs_hbm.at[0], rs, in_sem.at[1]),
        pltpu.make_async_copy(ls_hbm.at[0], ls, in_sem.at[2]),
    ]
    for copy in loads:
        copy.start()
    barrier = pltpu.get_barrier_semaphore()
    greeted = [to_y(d) for d in YORD] + [to_z(e) for e in ZORD] + [to_x(d) for d in XORD] + [twin]
    for device in greeted:
        pl.semaphore_signal(barrier, inc=1, device_id=device, device_id_type=MESH)

    sx, sl = {}, {}

    def right_over_x(q):
        for k in range(NCH):
            for d in XORD:
                at = pl.multiple_of(at_x(d) * XS, 8)
                sx[q, k, d] = remote(
                    rp.at[q, pl.ds(at, CR), :], xr.at[q, k, d - 1],
                    x_s.at[q, k, d - 1], x_r.at[q, k, d - 1], to_x(d),
                )

    parts = {}

    def take(q):
        cols = slice(q * BLK, (q + 1) * BLK)
        tile = g[:, cols]
        parts[q] = split(tile), split(tile.T)
        gs[0, :, cols], gs[1, :, cols] = parts[q][0]

    def right_gram(q):
        held, turned = parts[q]
        pack(rp.at[q], mm(turned, held))

    def start_x(q):
        for d in XORD:
            sx[q, 0, d].start()

    right_over_x(0)
    right_over_x(1)
    loads[0].wait()
    take(0)
    right_gram(0)
    pl.semaphore_wait(barrier, len(greeted))
    pl.when(core == 1)(lambda: start_x(0))
    loads[1].wait()
    take(1)
    pack(lp, mm(*parts[0]) + mm(*parts[1]))
    for d in YORD:
        at = pl.multiple_of(at_y(d) * YS, 8)
        sl[d] = send(lp.at[pl.ds(at, LP), :], lrecv.at[d - 1], ly_s.at[d - 1], ly_r.at[d - 1], to_y(d))
    right_gram(1)
    pl.when(core == 0)(lambda: pl.semaphore_wait(go_sem, 1))
    pl.when(core == 0)(lambda: start_x(0))
    start_x(1)

    sz = {}

    def right_over_z(q):
        for k in range(NCH):
            total = rp[q, pl.ds(pl.multiple_of(x * XS, 8), CR), :]
            for d in XORD:
                sx[q, k, d].wait_recv()
                total = total + xr[q, k, d - 1]
            zs[q, k] = total
            for e in ZORD:
                sz[q, k, e] = send(
                    zs.at[q, k], zr.at[q, k, e - 1], z_s.at[q, k, e - 1], z_r.at[q, k, e - 1], to_z(e)
                )

    gx = {}

    def right_gather(q):
        for k in range(NCH):
            total = zs[q, k]
            for e in (1, 3, 2):
                sz[q, k, e].wait_recv()
                total = total + zr[q, k, e - 1]
            rag[q, x] = total
            for d in XORD:
                gx[q, k, d] = send(
                    rag.at[q, x], rag.at[q, x], gx_s.at[q, k, d - 1], gx_r.at[q, k, d - 1], to_x(d)
                )

    right_over_z(0)

    @pl.when(core == 1)
    def _():
        pl.semaphore_signal(go_sem, inc=1, device_id=twin, device_id_type=MESH)

    right_over_z(1)

    at = pl.multiple_of(col * YS, 8)
    total = lp[pl.ds(at, LP), :]
    for d in YORD:
        sl[d].wait_recv()
        total = total + lrecv[d - 1]
    lag[col] = total
    sg = {}
    for d in YORD:
        sg[d] = send(lag.at[col], lag.at[col], lg_s.at[d - 1], lg_r.at[d - 1], to_y(d))

    def left_arrived():
        for d in YORD:
            sg[d].wait_recv()

    def right_arrived(q):
        for k in range(NCH):
            for d in XORD:
                gx[q, k, d].wait_recv()

    def stats_of(q):
        return unpack(rag.at[q], XS), rs[q * BLK : (q + 1) * BLK, :]

    su = {}

    def emit(q, root):
        cols = slice(q * BLK, (q + 1) * BLK)
        upd[q] = mm(split(hs[:, cols]), split(root))
        lanes = pl.ds(pl.multiple_of(col * 2 * BLK + q * BLK, BLK), BLK)
        for d in YORD:
            at = pl.multiple_of(at_y(d) * 32, 32)
            su[q, d] = send(
                upd.at[q, pl.ds(at, 32), :], o_ref.at[0, :, lanes], u_s.at[q, d - 1], u_r.at[q, d - 1], to_y(d)
            )
        mine = pltpu.make_async_copy(
            upd.at[q, pl.ds(pl.multiple_of(col * 32, 32), 32), :], o_ref.at[0, :, lanes], out_sem.at[q]
        )
        mine.start()
        su[q, 0] = mine

    loads[2].wait()
    loads[3].wait()
    right_gather(0)

    @pl.when(core == 0)
    def _():
        left_arrived()
        (left,) = newton((unpack(lag, YS), ls[...]))
        hs[...] = mm(split(left), (gs[0], gs[1]))

    right_gather(1)
    right_arrived(0)

    @pl.when(core == 0)
    def _():
        (rr[...],) = newton(stats_of(0))

    @pl.when(core == 1)
    def _():
        left_arrived()
        left, rr[...] = newton((unpack(lag, YS), ls[...]), stats_of(0))
        hs[...] = mm(split(left), (gs[0], gs[1]))

    emit(0, rr[...])
    right_arrived(1)
    (right,) = newton(stats_of(1))
    emit(1, right)

    for q in range(2):
        su[q, 0].wait()
        for d in YORD:
            su[q, d].wait_recv()
    for group in (sx, sl, sz, sg, gx):
        for copy in group.values():
            copy.wait_send()
    for (q, d), copy in su.items():
        if d:
            copy.wait_send()


def per_device(grads, left_stats, right_stats):
    dma = pltpu.SemaphoreType.DMA
    return pl.pallas_call(
        kernel,
        out_shape=pltpu.VMEM((1, 32, D), F32),
        in_specs=[pl.BlockSpec(memory_space=pl.ANY)] * 3,
        out_specs=pl.BlockSpec(memory_space=pltpu.VMEM),
        scratch_shapes=[
            pltpu.VMEM((BLK, 2 * BLK), F32),
            pltpu.VMEM((BLK, BLK), F32),
            pltpu.VMEM((2 * BLK, BLK), F32),
            pltpu.VMEM((2, BLK, 2 * BLK), BF16),
            pltpu.VMEM((BLK, 2 * BLK), F32),
            pltpu.VMEM((BLK, BLK), F32),
            pltpu.VMEM((PACK, H), F32),
            pltpu.VMEM((2, PACK, H), F32),
            pltpu.VMEM((NY - 1, LP, H), F32),
            pltpu.VMEM((2, NCH, NX - 1, CR, H), F32),
            pltpu.VMEM((2, NCH, CR, H), F32),
            pltpu.VMEM((2, NCH, NZ - 1, CR, H), F32),
            pltpu.VMEM((NY, LP, H), F32),
            pltpu.VMEM((2, NX, CR, H), F32),
            pltpu.VMEM((2, BLK, BLK), F32),
            pltpu.SemaphoreType.REGULAR,
            dma((4,)), dma((2,)),
            dma((NY - 1,)), dma((NY - 1,)), dma((NY - 1,)), dma((NY - 1,)),
            dma((2, NCH, NX - 1)), dma((2, NCH, NX - 1)),
            dma((2, NCH, NZ - 1)), dma((2, NCH, NZ - 1)),
            dma((2, NCH, NX - 1)), dma((2, NCH, NX - 1)),
            dma((2, NY - 1)), dma((2, NY - 1)),
        ],
        compiler_params=pltpu.CompilerParams(collective_id=0, has_side_effects=True),
        name="shampoo",
    )(grads, left_stats, right_stats)


def solution(mesh):
    return jax.shard_map(
        per_device,
        mesh=mesh,
        in_specs=(P("mat", "row", "col"), P("mat", "row", None), P("mat", "col", None)),
        out_specs=P("mat", ("row", "col"), None),
        check_vma=False,
    )
```
